32 devices in a mesh: ctx: 2 (over core), rep: 4 (over y, x), tp: 4 (over z).
Axes of the slice: x: 2, y: 2, z: 4, core: 2. Of those that a mesh axis runs over, the one named last changes fastest.
Arguments:
- prompt_x: bfloat16 [2048, 16384], P(('ctx', 'rep'), 'tp'), may hold values from -6 to 6
- prompt_z: bfloat16 [2048, 16384], P(('ctx', 'rep'), 'tp'), may hold values from -6 to 6
- prompt_b: bfloat16 [2048, 1024], P(('ctx', 'rep'), 'tp'), may hold values from -1.25 to 1.25
- prompt_c: bfloat16 [2048, 1024], P(('ctx', 'rep'), 'tp'), may hold values from -1.25 to 1.25
- prompt_dt: float32 [2048, 256], P(('ctx', 'rep'), 'tp'), may hold values from 0.2 to 1.2
- rate_log: float32 [256], P('tp'), may hold values from -30 to -2
- skip_scale: float32 [256], P('tp'), may hold values from 0.5 to 1.5
- norm_gain: float32 [16384], P('tp'), may hold values from 0.5 to 1.5
- prefix_key_rows: bfloat16 [2048, 1024], P(('ctx', 'rep'), 'tp'), may hold values from -6 to 6
- prefix_value_rows: bfloat16 [2048, 1024], P(('ctx', 'rep'), 'tp'), may hold values from -6 to 6
- fork_counts: int32 [8], P(('ctx', 'rep')), may hold values from 0 to 2, as said below
- fork_x: bfloat16 [16, 4, 16384], P(('ctx', 'rep'), None, 'tp'), may hold values from -6 to 6
- fork_z: bfloat16 [16, 4, 16384], P(('ctx', 'rep'), None, 'tp'), may hold values from -6 to 6
- fork_b: bfloat16 [16, 4, 1024], P(('ctx', 'rep'), None, 'tp'), may hold values from -1.25 to 1.25
- fork_c: bfloat16 [16, 4, 1024], P(('ctx', 'rep'), None, 'tp'), may hold values from -1.25 to 1.25
- fork_dt: float32 [16, 4, 256], P(('ctx', 'rep'), None, 'tp'), may hold values from 0.2 to 1.2
- fork_queries: bfloat16 [16, 4, 8192], P(('ctx', 'rep'), None, 'tp'), may hold values from -16 to 16
- fork_keys: bfloat16 [16, 4, 1024], P(('ctx', 'rep'), None, 'tp'), may hold values from -16 to 16
- branch_value_rows: bfloat16 [16, 4, 1024], P(('ctx', 'rep'), None, 'tp'), may hold values from -6 to 6
Outputs:
- prompt_out: bfloat16 [2048, 16384], P(('ctx', 'rep'), 'tp')
- fork_mamba: bfloat16 [16, 4, 16384], P(('ctx', 'rep'), None, 'tp')
- fork_attn: bfloat16 [16, 4, 8192], P(('ctx', 'rep'), None, 'tp')
The draws below stay inside these ranges and needn't reach their ends.
Inputs may be any that keep to these rules, and one draw needn't show every extreme that they name: `fork_counts`: after each segment at most 2 forks branch off; in every draw some segment has exactly 2.
All inputs are finite; a program needn't handle non-finite values.
Results may differ from the reference program's by a relative error of at most 0.00155.
Values may be sent and summed in bfloat16 or wider, within the bound.
A program may use at most 384 MiB of HBM per device.

```python
import math
import jax
import jax.numpy as jnp
from jax import lax

H = 256
P_SIZE = 64
N = 128
G = 8
QUERY_HEADS = 64
KEY_VALUE_HEADS = 8
HEAD_DIMENSION = 128
TOK_DEV = 256
SEGMENT_SLOTS = 2
FORK_STEPS = 4
SEGMENTS = 8
PROMPT_TOKENS = 2048
TOTAL_SLOTS = 16
N_CTX = 2
N_REP = 4


def draw_rate_log(key, part):
    fast_end = jnp.log(0.08)
    slow_end = jnp.log(0.5 / PROMPT_TOKENS)
    spread = jax.random.uniform(jax.random.fold_in(key, 5), (H,), jnp.float32)
    return (slow_end + spread * (fast_end - slow_end)).astype(jnp.float32)


def draw_fork_counts(key, part):
    counts_drawn = jax.random.randint(jax.random.fold_in(key, 7), (SEGMENTS,), 0, SEGMENT_SLOTS + 1)
    fullest = jax.random.randint(jax.random.fold_in(key, 8), (), 0, SEGMENTS)
    return counts_drawn.at[fullest].set(SEGMENT_SLOTS).astype(jnp.int32)


def attention_pair(key):
    query_matrix = jax.random.normal(jax.random.fold_in(key, 21), (TOTAL_SLOTS, FORK_STEPS, QUERY_HEADS * HEAD_DIMENSION), jnp.float32)
    query_matrix = jnp.clip(query_matrix, -16.0, 16.0)
    leading_slots = query_matrix.reshape(TOTAL_SLOTS, FORK_STEPS, KEY_VALUE_HEADS, QUERY_HEADS // KEY_VALUE_HEADS, HEAD_DIMENSION)[:, :, :, 0, :]
    random_portion = jax.random.normal(jax.random.fold_in(key, 23), (TOTAL_SLOTS, FORK_STEPS, KEY_VALUE_HEADS, HEAD_DIMENSION), jnp.float32)
    self_key_rows = jnp.clip(0.6 * leading_slots + 0.8 * random_portion, -16.0, 16.0).reshape(TOTAL_SLOTS, FORK_STEPS, KEY_VALUE_HEADS * HEAD_DIMENSION)
    return (query_matrix, self_key_rows)


def draw_fork_queries(key, part):
    return attention_pair(key)[0].astype(jnp.bfloat16)


def draw_fork_keys(key, part):
    return attention_pair(key)[1].astype(jnp.bfloat16)


def steps_of(stream_key, dims, shards, least, largest):
    def one(dim, shards_of):
        steps = jax.random.uniform(jax.random.fold_in(jax.random.fold_in(stream_key, 6), dim), (shards_of,), jnp.float32, least / len(shards), largest / len(shards))
        return jnp.repeat(jnp.exp(steps), dims[dim] // shards_of).reshape((-1,) + (1,) * (len(dims) - dim - 1))

    factor_of = one(*shards[0])
    for cut in shards[1:]:
        factor_of = factor_of * one(*cut)
    return factor_of


def normal_values(stream_key, shape, deviation, bound, cuts=(), dtype=jnp.bfloat16):
    entries = jax.random.normal(stream_key, shape, jnp.float32) * deviation
    if len(cuts) > 0:
        entries = steps_of(stream_key, shape, cuts, -0.22, 0.18) * entries
    return jnp.clip(entries, min=-bound, max=bound).astype(dtype)


def setup_inputs(seed: int = 0) -> dict:
    seeds = jax.random.split(jax.random.key(seed), 20)
    return {
        "prompt_x": normal_values(seeds[0], (PROMPT_TOKENS, H * P_SIZE), 1.0, 6.0, ((0, 8), (1, 4))),
        "prompt_z": normal_values(seeds[1], (PROMPT_TOKENS, H * P_SIZE), 1.0, 6.0, ((0, 8), (1, 4))),
        "prompt_b": normal_values(seeds[2], (PROMPT_TOKENS, G * N), (N ** -0.5), 1.25, ((0, 8), (1, 4))),
        "prompt_c": normal_values(seeds[3], (PROMPT_TOKENS, G * N), (N ** -0.5), 1.25, ((0, 8), (1, 4))),
        "prompt_dt": jnp.clip(jnp.exp(math.log(1.2) - 1.7917595 * jax.random.uniform(seeds[4], (PROMPT_TOKENS, H), jnp.float32) ** steps_of(seeds[4], (PROMPT_TOKENS, H), ((0, 8), (1, 4)), -0.2, 0.2)), 0.2, 1.2),
        "rate_log": draw_rate_log(jax.random.fold_in(seeds[19], 71), 0),
        "skip_scale": jnp.clip(0.5 + 1.0 * jax.random.uniform(seeds[6], (H,), jnp.float32) ** steps_of(seeds[6], (H,), ((0, 4),), -0.2, 0.2), 0.5, 1.5),
        "norm_gain": jnp.clip(1.0 + 0.1 * jax.random.normal(seeds[7], (H * P_SIZE,), jnp.float32), 0.5, 1.5),
        "prefix_key_rows": normal_values(seeds[8], (PROMPT_TOKENS, KEY_VALUE_HEADS * HEAD_DIMENSION), 1.0, 6.0, ((0, 8), (1, 4))),
        "prefix_value_rows": normal_values(seeds[9], (PROMPT_TOKENS, KEY_VALUE_HEADS * HEAD_DIMENSION), 1.0, 6.0, ((0, 8), (1, 4))),
        "fork_counts": draw_fork_counts(jax.random.fold_in(seeds[19], 71), 0),
        "fork_x": normal_values(seeds[11], (TOTAL_SLOTS, FORK_STEPS, H * P_SIZE), 1.0, 6.0, ((0, 8), (2, 4))),
        "fork_z": normal_values(seeds[12], (TOTAL_SLOTS, FORK_STEPS, H * P_SIZE), 1.0, 6.0, ((0, 8), (2, 4))),
        "fork_b": normal_values(seeds[13], (TOTAL_SLOTS, FORK_STEPS, G * N), (N ** -0.5), 1.25, ((0, 8), (2, 4))),
        "fork_c": normal_values(seeds[14], (TOTAL_SLOTS, FORK_STEPS, G * N), (N ** -0.5), 1.25, ((0, 8), (2, 4))),
        "fork_dt": jnp.clip(jnp.exp(math.log(1.2) - 1.7917595 * jax.random.uniform(seeds[15], (TOTAL_SLOTS, FORK_STEPS, H), jnp.float32) ** steps_of(seeds[15], (TOTAL_SLOTS, FORK_STEPS, H), ((0, 8), (2, 4)), -0.2, 0.2)), 0.2, 1.2),
        "fork_queries": draw_fork_queries(jax.random.fold_in(seeds[19], 71), 0),
        "fork_keys": draw_fork_keys(jax.random.fold_in(seeds[19], 71), 0),
        "branch_value_rows": normal_values(seeds[18], (TOTAL_SLOTS, FORK_STEPS, KEY_VALUE_HEADS * HEAD_DIMENSION), 1.0, 6.0, ((0, 8), (2, 4))),
    }


HIGHEST = lax.Precision.HIGHEST
EPSILON = 1e-05

def expand_groups(values, head_count, state_depth):
    leading = values.shape[:-1]
    groups = values.shape[-1] // state_depth
    shaped = values.reshape(leading + (groups, state_depth))
    return jnp.repeat(shaped, head_count // groups, axis=len(leading)).astype(jnp.float32)

def ssd_block(state_now, block_x, block_b, block_c, block_dt, decay_rates, skip_scale):
    length, head_count = block_dt.shape
    head_width, state_depth = (state_now.shape[1], state_now.shape[2])
    groups = block_b.shape[1] // state_depth
    cumulated = jnp.cumsum(block_dt * decay_rates[None, :], axis=0)
    x_heads = block_x.reshape(length, head_count, head_width).astype(jnp.float32)
    inputs = x_heads * block_dt[:, :, None]
    pairing = jnp.einsum('tgn,sgn->gts', block_c.reshape(length, groups, state_depth), block_b.reshape(length, groups, state_depth), preferred_element_type=jnp.float32)
    pairing = jnp.repeat(pairing, head_count // groups, axis=0)
    log_gaps = cumulated.T[:, :, None] - cumulated.T[:, None, :]
    lower_mask = (jnp.arange(length)[:, None] >= jnp.arange(length)[None, :])[None]
    mixing = jnp.where(lower_mask, jnp.exp(jnp.where(lower_mask, log_gaps, 0.0)), 0.0) * pairing
    inside = jnp.einsum('hts,shp->thp', mixing, inputs, precision=HIGHEST)
    c_heads = expand_groups(block_c, head_count, state_depth)
    b_heads = expand_groups(block_b, head_count, state_depth)
    carried = jnp.einsum('thn,hpn->thp', c_heads, state_now, precision=HIGHEST) * jnp.exp(cumulated)[:, :, None]
    output = inside + carried + skip_scale[None, :, None] * x_heads
    remaining = jnp.exp(cumulated[-1][None, :] - cumulated)
    fresh_part = jnp.einsum('shp,shn->hpn', inputs * remaining[:, :, None], b_heads, precision=HIGHEST)
    new_state = jnp.exp(cumulated[-1])[:, None, None] * state_now + fresh_part
    return (new_state, output, c_heads)

def fork_update(fork_state, step_x, step_b, step_c, step_dt, decay_rates, skip_scale):
    slot_count, head_count = step_dt.shape
    head_width, state_depth = (fork_state.shape[2], fork_state.shape[3])
    x_heads = step_x.reshape(slot_count, head_count, head_width).astype(jnp.float32)
    b_heads = expand_groups(step_b, head_count, state_depth)
    c_heads = expand_groups(step_c, head_count, state_depth)
    decays = jnp.exp(step_dt * decay_rates[None, :])
    fork_state = decays[:, :, None, None] * fork_state + (x_heads * step_dt[:, :, None])[:, :, :, None] * b_heads[:, :, None, :]
    output = jnp.einsum('mhpn,mhn->mhp', fork_state, c_heads, precision=HIGHEST) + skip_scale[None, :, None] * x_heads
    return (fork_state, output)

def gate_terms(output, gate_in):
    return output * jax.nn.silu(gate_in.astype(jnp.float32).reshape(output.shape))

def normalize(gated, gain_table):
    mean_square = lax.optimization_barrier(jnp.mean(gated * gated, axis=(-2, -1)))
    return gated * lax.rsqrt(mean_square + EPSILON)[..., None, None] * gain_table

def reference(prompt_x, prompt_z, prompt_b, prompt_c, prompt_dt, rate_log, skip_scale, norm_gain, prefix_key_rows, prefix_value_rows, fork_counts, fork_x, fork_z, fork_b, fork_c, fork_dt, fork_queries, fork_keys, branch_value_rows):
    decay_rates = -jnp.exp(rate_log)
    segment_count = N_CTX * N_REP
    block_rows = min(128, TOK_DEV)
    gain_table = norm_gain.reshape(H, P_SIZE)
    query_group_width = QUERY_HEADS // KEY_VALUE_HEADS
    score_scale = HEAD_DIMENSION ** (-0.5)
    joined_keys = prefix_key_rows.reshape(PROMPT_TOKENS, KEY_VALUE_HEADS, HEAD_DIMENSION)
    joined_values = prefix_value_rows.reshape(PROMPT_TOKENS, KEY_VALUE_HEADS, HEAD_DIMENSION).astype(jnp.float32)
    positions = jnp.arange(PROMPT_TOKENS)
    causal_mask = (jnp.arange(FORK_STEPS)[:, None] >= jnp.arange(FORK_STEPS)[None, :])[None, None, :, None, :]

    def per_segment(values):
        return values.reshape((segment_count, values.shape[0] // segment_count) + values.shape[1:])

    def segment_step(state_now, inputs):
        seg_index, seg_x, seg_z, seg_b, seg_c, seg_dt, fork_count, slot_x, slot_z, slot_b, slot_c, slot_dt, slot_query_rows, slot_key_rows, slot_value_rows = inputs
        pieces = []
        for block_start in range(0, TOK_DEV, block_rows):
            block_end = block_start + block_rows
            state_now, output, c_heads = ssd_block(state_now, seg_x[block_start:block_end], seg_b[block_start:block_end], seg_c[block_start:block_end], seg_dt[block_start:block_end], decay_rates, skip_scale)
            pieces.append(output)
        prompt_gated = gate_terms(jnp.concatenate(pieces, axis=0), seg_z)
        prompt_rows = normalize(prompt_gated, gain_table).astype(jnp.bfloat16).reshape(TOK_DEV, H * P_SIZE)
        live_slots = (jnp.arange(SEGMENT_SLOTS) < fork_count).astype(jnp.float32)
        fork_state = jnp.broadcast_to(state_now, (SEGMENT_SLOTS,) + state_now.shape)
        gated_steps = []
        for step_index in range(FORK_STEPS):
            fork_state, output = fork_update(fork_state, slot_x[:, step_index], slot_b[:, step_index], slot_c[:, step_index], slot_dt[:, step_index], decay_rates, skip_scale)
            gated_steps.append(gate_terms(output, slot_z[:, step_index]))
        fork_gated = jnp.stack(gated_steps, axis=1)
        mamba_rows = (normalize(fork_gated, gain_table) * live_slots[:, None, None, None]).astype(jnp.bfloat16).reshape(SEGMENT_SLOTS, FORK_STEPS, H * P_SIZE)
        query_matrix = slot_query_rows.reshape(SEGMENT_SLOTS, FORK_STEPS, KEY_VALUE_HEADS, query_group_width, HEAD_DIMENSION)
        key_limit = (seg_index + 1) * TOK_DEV
        prompt_scores = jnp.einsum('msgqd,tgd->gmsqt', query_matrix, joined_keys, preferred_element_type=jnp.float32) * score_scale
        prompt_scores = jnp.where(positions < key_limit, prompt_scores, -jnp.inf)
        self_key_rows = slot_key_rows.reshape(SEGMENT_SLOTS, FORK_STEPS, KEY_VALUE_HEADS, HEAD_DIMENSION)
        self_value_rows = slot_value_rows.reshape(SEGMENT_SLOTS, FORK_STEPS, KEY_VALUE_HEADS, HEAD_DIMENSION).astype(jnp.float32)
        own_scores = jnp.einsum('msgqd,mtgd->gmsqt', query_matrix, self_key_rows, preferred_element_type=jnp.float32) * score_scale
        own_scores = jnp.where(causal_mask, own_scores, -jnp.inf)
        peak_score = jnp.maximum(lax.optimization_barrier(jnp.max(prompt_scores, axis=-1)), lax.optimization_barrier(jnp.max(own_scores, axis=-1)))
        prompt_weights = jnp.exp(prompt_scores - peak_score[..., None])
        own_weights = jnp.exp(own_scores - peak_score[..., None])
        weight_sum = lax.optimization_barrier(jnp.sum(prompt_weights, axis=-1)) + lax.optimization_barrier(jnp.sum(own_weights, axis=-1))
        weighted = jnp.einsum('gmsqt,tgd->gmsqd', prompt_weights, joined_values, precision=HIGHEST) + jnp.einsum('gmsqt,mtgd->gmsqd', own_weights, self_value_rows, precision=HIGHEST)
        attended = weighted / weight_sum[..., None]
        attn_rows = (jnp.transpose(attended, (1, 2, 0, 3, 4)) * live_slots[:, None, None, None, None]).astype(jnp.bfloat16).reshape(SEGMENT_SLOTS, FORK_STEPS, QUERY_HEADS * HEAD_DIMENSION)
        return (state_now, (prompt_rows, mamba_rows, attn_rows))
    sequence = (jnp.arange(segment_count), per_segment(prompt_x), per_segment(prompt_z), per_segment(prompt_b), per_segment(prompt_c), per_segment(prompt_dt), fork_counts, per_segment(fork_x), per_segment(fork_z), per_segment(fork_b), per_segment(fork_c), per_segment(fork_dt), per_segment(fork_queries), per_segment(fork_keys), per_segment(branch_value_rows))
    start_state = jnp.zeros((H, P_SIZE, N), jnp.float32)
    final_state, results = lax.scan(segment_step, start_state, sequence)
    prompt_rows, mamba_rows, attn_rows = results
    return (prompt_rows.reshape(PROMPT_TOKENS, H * P_SIZE), mamba_rows.reshape(TOTAL_SLOTS, FORK_STEPS, H * P_SIZE), attn_rows.reshape(TOTAL_SLOTS, FORK_STEPS, QUERY_HEADS * HEAD_DIMENSION))
```

```python
import jax
import jax.numpy as jnp
from jax import lax
from jax.sharding import PartitionSpec as P

P_SIZE = 64
N = 128
HEAD_DIMENSION = 128
EPSILON = 1e-05
FLOOR_SCORE = -1e30
SEG = ("ctx", "rep")
BF = jnp.bfloat16
F32 = jnp.float32


def dot(a, b, dims=((1,), (0,))):
    return lax.dot_general(a, b, (dims, ((), ())), preferred_element_type=F32)


def split2(a):
    hi = a.astype(BF)
    return hi, (a - hi.astype(F32)).astype(BF)


def split3(a):
    hi = a.astype(BF)
    rest = a - hi.astype(F32)
    mid = rest.astype(BF)
    return hi, mid, (rest - mid.astype(F32)).astype(BF)


def mm_right(a, b, dims=((1,), (0,))):
    hi, lo = split2(b)
    return dot(a, hi, dims) + dot(a, lo, dims)


def mm_left(a, b, dims=((1,), (0,))):
    hi, lo = split2(a)
    return dot(hi, b, dims) + dot(lo, b, dims)


def mm_both(a, b):
    ah, al = split2(a)
    bh, bl = split2(b)
    return dot(ah, bh) + (dot(ah, bl) + dot(al, bh))


def spread(values, table):
    parts = split3(values)
    return dot(parts[0], table) + (dot(parts[1], table) + dot(parts[2], table))


def spread_table(heads):
    row = lax.broadcasted_iota(jnp.int32, (heads, heads * P_SIZE), 0)
    col = lax.broadcasted_iota(jnp.int32, (heads, heads * P_SIZE), 1)
    return jnp.where(col // P_SIZE == row, 1.0, 0.0).astype(BF)


def causal(rows, span):
    r = lax.broadcasted_iota(jnp.int32, (rows, rows), 0)
    c = lax.broadcasted_iota(jnp.int32, (rows, rows), 1)
    return (r >= c) & (r // span == c // span)


def block_terms(x, b, c, dt, rates, span, table):
    rows = x.shape[0]
    mask = causal(rows, span)
    ones = mask.astype(F32).astype(BF)
    parts = split3(dt * rates)
    cum = dot(ones, parts[0]) + (dot(ones, parts[1]) + dot(ones, parts[2]))
    xs = x.astype(F32) * spread(dt * jnp.exp(-cum), table)
    groups = b.shape[1] // N
    width = x.shape[1] // groups
    inside = []
    for g in range(groups):
        pair = dot(c[:, g * N : (g + 1) * N], b[:, g * N : (g + 1) * N], ((1,), (1,)))
        pair = jnp.where(mask, pair, 0.0)
        inside.append(mm_both(pair, xs[:, g * width : (g + 1) * width]))
    return cum, xs, inside


def encode(chunk, axis):
    scale = jnp.maximum(jnp.max(jnp.abs(chunk), axis=axis, keepdims=True), 1e-30)
    code = jnp.round(chunk * (32767.0 / scale)).astype(jnp.int16)
    return code, scale * (1.0 / 32767.0)


def gate(y, z):
    z = z.astype(F32)
    return y * (z / (1.0 + jnp.exp(-z)))


def swap(values, axes):
    return lax.all_to_all(values, axes, split_axis=0, concat_axis=0, tiled=True)


def attend_part(queries, keys, values, live, kv, q_per):
    rows = queries.shape[0]
    scale = HEAD_DIMENSION ** (-0.5)
    out, peaks, sums = [], [], []
    D = HEAD_DIMENSION
    for k in range(kv):
        q = jnp.concatenate(
            [queries[:, (k * q_per + i) * D : (k * q_per + i + 1) * D] for i in range(q_per)], axis=0
        )
        s = dot(q, keys[:, k * D : (k + 1) * D], ((1,), (1,))) * scale
        s = jnp.where(live, s, FLOOR_SCORE)
        m = jnp.max(s, axis=1, keepdims=True)
        w = jnp.where(live, jnp.exp(s - m), 0.0)
        o = mm_left(w, values[:, k * D : (k + 1) * D])
        l = jnp.sum(w, axis=1, keepdims=True)
        for i in range(q_per):
            out.append(o[i * rows : (i + 1) * rows])
            peaks.append(m[i * rows : (i + 1) * rows])
            sums.append(l[i * rows : (i + 1) * rows])
    return out, peaks, sums


def on_device(
    prompt_x,
    prompt_z,
    prompt_b,
    prompt_c,
    prompt_dt,
    rate_log,
    skip_scale,
    norm_gain,
    prefix_key_rows,
    prefix_value_rows,
    fork_counts,
    fork_x,
    fork_z,
    fork_b,
    fork_c,
    fork_dt,
    fork_queries,
    fork_keys,
    branch_value_rows,
):
    slots, steps = fork_x.shape[:2]
    forks = slots * steps
    flat = lambda a: a.reshape(forks, a.shape[2])
    fx, fz, fb, fc, fdt, fq, fk, fv = map(
        flat, (fork_x, fork_z, fork_b, fork_c, fork_dt, fork_queries, fork_keys, branch_value_rows)
    )
    me = lax.axis_index(SEG)
    n_seg = lax.axis_size(SEG)
    n_tp = lax.axis_size("tp")
    tok, channels = prompt_x.shape
    heads = rate_log.shape[0]
    groups = prompt_b.shape[1] // N
    width = channels // groups
    kv = prefix_key_rows.shape[1] // HEAD_DIMENSION
    q_per = fq.shape[1] // HEAD_DIMENSION // kv
    rates = -jnp.exp(rate_log)[None, :]
    table = spread_table(heads)
    lane_parts = min(n_seg, channels // 128)
    row_parts = n_seg // lane_parts
    lanes, rows = channels // lane_parts, N // row_parts

    def cut(a):
        a = a.reshape(row_parts, rows, lane_parts, lanes)
        return jnp.transpose(a, (0, 2, 1, 3)).reshape(n_seg, rows, lanes)

    def join(a):
        a = a.reshape(row_parts, lane_parts, rows, lanes)
        return jnp.transpose(a, (0, 2, 1, 3)).reshape(N, channels)

    every_query = swap(jnp.broadcast_to(fq[None], (n_seg,) + fq.shape), SEG)
    cum, xs, inside = block_terms(prompt_x, prompt_b, prompt_c, prompt_dt, rates, tok, table)
    state = jnp.concatenate(
        [
            mm_right(prompt_b[:, g * N : (g + 1) * N], xs[:, g * width : (g + 1) * width], ((0,), (0,)))
            for g in range(groups)
        ],
        axis=1,
    )
    last = spread(jnp.exp(cum[-1:]), table)
    state = state * last
    codes, scales = encode(cut(state), 1)
    codes = swap(codes, SEG)
    decay = jnp.broadcast_to(last.reshape(1, lane_parts, 1, lanes), (row_parts, lane_parts, 1, lanes))
    side = swap(jnp.concatenate([scales, decay.reshape(n_seg, 1, lanes)], axis=1), SEG)
    run = jnp.zeros((rows, lanes), F32)
    entering = []
    for e in range(n_seg):
        entering.append(run)
        run = run * side[e, 1:2] + codes[e].astype(F32) * side[e, 0:1]
    codes, scales = encode(jnp.stack(entering), 1)
    codes = swap(codes, SEG)
    scales = swap(scales, SEG)
    before = join(codes.astype(F32) * scales)

    aq = every_query.reshape(n_seg * forks, fq.shape[1])
    owner = lax.broadcasted_iota(jnp.int32, (q_per, n_seg * forks, 1), 1) // forks
    live = (owner >= me).reshape(q_per * n_seg * forks, 1)
    out, peaks, sums = attend_part(aq, prefix_key_rows, prefix_value_rows, live, kv, q_per)
    pad = jnp.zeros((n_seg * forks, 128 - 2 * kv * q_per), F32)
    packed = jnp.concatenate(out + peaks + sums + [pad], axis=1)
    packed = swap(packed.reshape(n_seg, forks, packed.shape[1]), SEG)

    fcum, fxs, finside = block_terms(fx, fb, fc, fdt, rates, steps, table)
    ys, fys = [], []
    for g in range(groups):
        lane = slice(g * width, (g + 1) * width)
        col = slice(g * N, (g + 1) * N)
        hi, lo = split2(before[:, lane])
        ys.append(inside[g] + dot(prompt_c[:, col], hi) + dot(prompt_c[:, col], lo))
        end = before[:, lane] * last[:, lane] + state[:, lane]
        fys.append(finside[g] + mm_right(fc[:, col], end))
    skip = spread(skip_scale[None, :], table)
    y = jnp.concatenate(ys, axis=1) * spread(jnp.exp(cum), table) + skip * prompt_x.astype(F32)
    fy = jnp.concatenate(fys, axis=1) * spread(jnp.exp(fcum), table) + skip * fx.astype(F32)
    gated = gate(y, prompt_z)
    fgated = gate(fy, fz)
    squares = jnp.concatenate([jnp.sum(gated * gated, axis=1), jnp.sum(fgated * fgated, axis=1)])
    squares = jnp.sum(swap(jnp.broadcast_to(squares[None], (n_tp,) + squares.shape), "tp"), axis=0)
    inv = lax.rsqrt(squares / (channels * n_tp) + EPSILON)[:, None]
    gain = norm_gain[None, :]
    alive = (lax.broadcasted_iota(jnp.int32, (forks, 1), 0) // steps < fork_counts[0]).astype(F32)
    prompt_out = (gated * inv[:tok] * gain).astype(BF)
    fork_mamba = (fgated * inv[tok:] * gain * alive).astype(BF)

    r = lax.broadcasted_iota(jnp.int32, (q_per * forks, forks), 0) % forks
    c = lax.broadcasted_iota(jnp.int32, (q_per * forks, forks), 1)
    own_live = (r >= c) & (r // steps == c // steps)
    own_out, own_peaks, own_sums = attend_part(fq, fk, fv, own_live, kv, q_per)
    hq = kv * q_per
    D = HEAD_DIMENSION
    results = []
    for h in range(hq):
        pk = packed[:, :, hq * D + h : hq * D + h + 1]
        sm = packed[:, :, hq * D + hq + h : hq * D + hq + h + 1]
        peak = jnp.maximum(jnp.max(pk, axis=0), own_peaks[h])
        factor = jnp.exp(pk - peak[None])
        own = jnp.exp(own_peaks[h] - peak)
        total = jnp.sum(sm * factor, axis=0) + own_sums[h] * own
        weighted = jnp.sum(packed[:, :, h * D : (h + 1) * D] * factor, axis=0) + own_out[h] * own
        results.append(weighted / total * alive)
    fork_attn = jnp.concatenate(results, axis=1).astype(BF)
    shape3 = lambda a: a.reshape(slots, steps, a.shape[1])
    return (prompt_out, shape3(fork_mamba), shape3(fork_attn))


def solution(mesh):
    rows = P(SEG, "tp")
    fork = P(SEG, None, "tp")
    in_specs = (rows,) * 5 + (P("tp"),) * 3 + (rows,) * 2 + (P(SEG),) + (fork,) * 8
    return jax.shard_map(
        on_device, mesh=mesh, in_specs=in_specs, out_specs=(rows, fork, fork), check_vma=False
    )
```

```python
import functools

import jax
import jax.numpy as jnp
from jax import lax
from jax.experimental import pallas as pl
from jax.experimental.pallas import tpu as pltpu
from jax.sharding import PartitionSpec as P

P_SIZE = 64
N = 128
HEAD_DIMENSION = 128
EPSILON = 1e-05
FLOOR_SCORE = -1e30
SEG = ("ctx", "rep")
BF = jnp.bfloat16
F32 = jnp.float32
VM = pltpu.VMEM


def dot(a, b, dims=((1,), (0,))):
    return lax.dot_general(a, b, (dims, ((), ())), preferred_element_type=F32)


def split2(a):
    hi = a.astype(BF)
    return hi, (a - hi.astype(F32)).astype(BF)


def split3(a):
    hi = a.astype(BF)
    rest = a - hi.astype(F32)
    mid = rest.astype(BF)
    return hi, mid, (rest - mid.astype(F32)).astype(BF)


def mm_right(a, b, dims=((1,), (0,))):
    hi, lo = split2(b)
    return dot(a, hi, dims) + dot(a, lo, dims)


def mm_left(a, b, dims=((1,), (0,))):
    hi, lo = split2(a)
    return dot(hi, b, dims) + dot(lo, b, dims)


def mm_both(a, b):
    ah, al = split2(a)
    bh, bl = split2(b)
    return dot(ah, bh) + (dot(ah, bl) + dot(al, bh))


def iota(shape, axis):
    return lax.broadcasted_iota(jnp.int32, shape, axis)


def log2(n):
    assert n & (n - 1) == 0
    return n.bit_length() - 1


def spread(values, table):
    return mm_left(values, table)


def spread_table(heads, step, width):
    row = iota((heads, width), 0) - step * (width // P_SIZE)
    col = iota((heads, width), 1)
    return jnp.where((col >= row * P_SIZE) & (col < row * P_SIZE + P_SIZE), 1.0, 0.0).astype(BF)


def causal(rows, span):
    r, c = iota((rows, rows), 0), iota((rows, rows), 1)
    mask = r >= c
    if span < rows:
        mask = mask & ((r >> log2(span)) == (c >> log2(span)))
    return mask


def running(dt, rates, span):
    ones = jnp.where(causal(dt.shape[0], span), 1.0, 0.0).astype(BF)
    parts = split3(dt * rates)
    return dot(ones, parts[0]) + (dot(ones, parts[1]) + dot(ones, parts[2]))


def encode(chunk):
    scale = jnp.maximum(jnp.max(jnp.abs(chunk), axis=0, keepdims=True), 1e-30)
    code = jnp.floor(chunk * (32767.0 / scale) + 0.5).astype(jnp.int32).astype(jnp.int16)
    return code, scale * (1.0 / 32767.0)


def decode(code, scale):
    return code.astype(jnp.int32).astype(F32) * scale


def gate(y, z):
    z = z.astype(F32)
    return y * (z / (1.0 + jnp.exp(-z)))


def first_kernel(steps, per_group, x, b, c, dt, rate, fx, fb, fc, fdt, codes, side, pre, fpre, cum, fcum, phi, plo, fpair):
    step = pl.program_id(0)
    tok, forks, heads, width = x.shape[0], fx.shape[0], dt.shape[1], x.shape[1]

    @pl.when(step == 0)
    def _():
        rates = -jnp.exp(rate[...])
        cum[...] = running(dt[...], rates, tok)
        fcum[...] = running(fdt[...], rates, steps)

    @pl.when(lax.rem(step, per_group) == 0)
    def _():
        pair = jnp.where(causal(tok, tok), dot(c[...], b[...], ((1,), (1,))), 0.0)
        phi[...], plo[...] = split2(pair)
        pair = jnp.where(causal(forks, steps), dot(fc[...], fb[...], ((1,), (1,))), 0.0)
        fpair[...] = pair

    table = spread_table(heads, step, width)
    total = cum[...]
    xs = x[...].astype(F32) * spread(dt[...] * jnp.exp(-total), table)
    xh, xl = split2(xs)
    pre[...] = dot(phi[...], xh) + (dot(phi[...], xl) + dot(plo[...], xh))
    last = spread(jnp.exp(total[tok - 8 :]), table)[7:8]
    state = (dot(b[...], xh, ((0,), (0,))) + dot(b[...], xl, ((0,), (0,)))) * last
    row_parts, lane_parts, rows, lanes = codes.shape
    for i in range(row_parts):
        for j in range(lane_parts):
            piece = state[i * rows : (i + 1) * rows, j * lanes : (j + 1) * lanes]
            codes[i, j], scale = encode(piece)
            side[i, j, 0:1] = scale
            side[i, j, 1:2] = last[:, j * lanes : (j + 1) * lanes]
            side[i, j, 2:8] = jnp.zeros((6, lanes), F32)
    fxs = fx[...].astype(F32) * spread(fdt[...] * jnp.exp(-fcum[...]), table)
    sh, sl = split2(state)
    inside = mm_both(fpair[...], fxs)
    fpre[...] = inside + dot(fc[...], sh) + dot(fc[...], sl)


def exchange_kernel(axes, n, whole, count, *refs):
    ins, outs = refs[:count], refs[count : 2 * count]
    send, recv = refs[2 * count :]
    me = lax.axis_index(axes)

    def place(j):
        if isinstance(axes, str):
            return {axes: j}
        inner = lax.axis_size(axes[1])
        return {axes[0]: j // inner, axes[1]: lax.rem(j, inner)}

    barrier = pltpu.get_barrier_semaphore()
    for s in range(1, n):
        pl.semaphore_signal(barrier, inc=1, device_id=place(lax.rem(me + s, n)), device_id_type=pl.DeviceIdType.MESH)
    pl.semaphore_wait(barrier, n - 1)
    copies = []
    for a in range(count):
        for s in range(1, n):
            peer = lax.rem(me + s, n)
            copies.append(
                pltpu.make_async_remote_copy(
                    src_ref=ins[a] if whole[a] else ins[a].at[peer],
                    dst_ref=outs[a].at[me],
                    send_sem=send.at[a, s - 1],
                    recv_sem=recv.at[a, s - 1],
                    device_id=place(peer),
                    device_id_type=pl.DeviceIdType.MESH,
                )
            )
            copies[-1].start()
    for a in range(count):
        outs[a][me] = ins[a][...] if whole[a] else ins[a][me]
    for copy in copies:
        copy.wait()


def exchange(arrays, whole, axes, n, number):
    shapes = [
        jax.ShapeDtypeStruct(((n,) + a.shape) if w else a.shape, a.dtype) for a, w in zip(arrays, whole)
    ]
    count = len(arrays)
    spec = pl.BlockSpec(memory_space=VM)
    return pl.pallas_call(
        functools.partial(exchange_kernel, axes, n, whole, count),
        out_shape=shapes,
        in_specs=[spec] * count,
        out_specs=[spec] * count,
        scratch_shapes=[pltpu.SemaphoreType.DMA((count, n - 1)), pltpu.SemaphoreType.DMA((count, n - 1))],
        compiler_params=pltpu.CompilerParams(collective_id=number, has_side_effects=True),
        name=f"exchange{number}",
    )(*arrays)


def attend(queries, keys, values, live):
    s = dot(queries, keys, ((1,), (1,))) * (HEAD_DIMENSION ** (-0.5))
    s = jnp.where(live, s, FLOOR_SCORE)
    m = jnp.max(s, axis=1, keepdims=True)
    w = jnp.where(live, jnp.exp(s - m), 0.0)
    return mm_left(w, values), m, jnp.sum(w, axis=1, keepdims=True)


def gather_heads(queries, k, q_per):
    D = HEAD_DIMENSION
    cols = [queries[:, (k * q_per + i) * D : (k * q_per + i + 1) * D].astype(F32) for i in range(q_per)]
    return jnp.concatenate(cols, axis=0).astype(BF)


def middle_kernel(forks, codes, side, queries, keys, values, ecodes, eside, packed):
    n_seg, rows, lanes = codes.shape
    D = HEAD_DIMENSION
    run = jnp.zeros((rows, lanes), F32)
    for e in range(n_seg):
        ecodes[e], scale = encode(run)
        eside[e] = jnp.broadcast_to(scale, (8, lanes))
        run = run * side[e, 1:2] + decode(codes[e], side[e, 0:1])
    me = lax.axis_index(SEG)
    kv = keys.shape[1] // D
    q_per = queries.shape[1] // D // kv
    count = queries.shape[0]
    shape = (q_per * count, keys.shape[0])
    live = ((iota(shape, 0) & (count - 1)) >> log2(forks)) >= me
    lane = iota((count, 128), 1)
    extra = jnp.zeros((count, 128), F32)
    for k in range(kv):
        o, m, l = attend(gather_heads(queries[...], k, q_per), keys[:, k * D : (k + 1) * D], values[:, k * D : (k + 1) * D], live)
        for i in range(q_per):
            h = k * q_per + i
            part = slice(i * count, (i + 1) * count)
            packed[:, h * D : (h + 1) * D] = o[part]
            extra = jnp.where(lane == h, m[part], extra)
            extra = jnp.where(lane == kv * q_per + h, l[part], extra)
    packed[:, kv * q_per * D :] = extra


def last_kernel(steps, x, z, c, dt, rate, skip, fx, fz, fc, fdt, codes, side, pre, fpre, gated, fgated, sq, cum, fcum):
    step = pl.program_id(0)
    tok, heads, width = x.shape[0], dt.shape[1], x.shape[1]

    @pl.when(step == 0)
    def _():
        rates = -jnp.exp(rate[...])
        cum[...] = running(dt[...], rates, tok)
        fcum[...] = running(fdt[...], rates, steps)
        sq[...] = jnp.zeros_like(sq)

    row_parts, lane_parts, rows, lanes = codes.shape
    before = jnp.concatenate(
        [
            jnp.concatenate([decode(codes[i, j], side[i, j, 0:1]) for j in range(lane_parts)], axis=1)
            for i in range(row_parts)
        ],
        axis=0,
    )
    table = spread_table(heads, step, width)
    grown = jnp.exp(cum[...])
    wide = spread(grown, table)
    skips = spread(jnp.broadcast_to(skip[...], (8, heads)), table)[0:1]
    hi, lo = split2(before)
    y = wide * (pre[...] + (dot(c[...], hi) + dot(c[...], lo))) + skips * x[...].astype(F32)
    g = gate(y, z[...])
    gated[...] = g
    gh, gl = split2(g * g)
    ones = jnp.ones((8, width), BF)
    sq[:, :tok] += dot(ones, gh, ((1,), (1,))) + dot(ones, gl, ((1,), (1,)))
    last = spread(grown[tok - 8 :], table)[7:8]
    fy = fpre[...] + last * (dot(fc[...], hi) + dot(fc[...], lo))
    fg = gate(spread(jnp.exp(fcum[...]), table) * fy + skips * fx[...].astype(F32), fz[...])
    fgated[...] = fg
    sq[:, tok:] += jnp.broadcast_to(jnp.sum(fg * fg, axis=1, keepdims=True), (fg.shape[0], 128))


def norm_kernel(steps, total, counts, gated, fgated, sq, gain, out, fout):
    tok, forks = gated.shape[0], fgated.shape[0]
    sums = sq[0]
    for i in range(1, sq.shape[0]):
        sums = sums + sq[i]
    inv = lax.rsqrt(sums * (1.0 / total) + EPSILON)
    column = jnp.transpose(inv[:, :tok])[:, 0:1]
    out[...] = (gated[...] * column * gain[...]).astype(BF)
    alive = jnp.where((iota((forks, 1), 0) >> log2(steps)) < counts[0], 1.0, 0.0)
    fout[...] = (fgated[...] * inv[:, tok : tok + 1] * gain[...] * alive).astype(BF)


def merge_kernel(steps, counts, packed, queries, keys, values, out):
    D = HEAD_DIMENSION
    forks = queries.shape[0]
    sources = packed.shape[0]
    kv = keys.shape[1] // D
    q_per = queries.shape[1] // D // kv
    heads = kv * q_per
    r = iota((q_per * forks, forks), 0) & (forks - 1)
    c = iota((q_per * forks, forks), 1)
    live = (r >= c) & ((r >> log2(steps)) == (c >> log2(steps)))
    alive = jnp.where((iota((forks, 1), 0) >> log2(steps)) < counts[0], 1.0, 0.0)
    extra = packed[:, :, heads * D :]
    for k in range(kv):
        o, m, l = attend(gather_heads(queries[...], k, q_per), keys[:, k * D : (k + 1) * D], values[:, k * D : (k + 1) * D], live)
        for i in range(q_per):
            h = k * q_per + i
            part = slice(i * forks, (i + 1) * forks)
            pk = extra[:, :, h : h + 1]
            peak = jnp.maximum(jnp.max(pk, axis=0), m[part])
            own = jnp.exp(m[part] - peak)
            total, weighted = l[part] * own, o[part] * own
            for e in range(sources):
                factor = jnp.exp(pk[e] - peak)
                total = total + extra[e, :, heads + h : heads + h + 1] * factor
                weighted = weighted + packed[e, :, h * D : (h + 1) * D] * factor
            out[:, h * D : (h + 1) * D] = (weighted / total * alive).astype(BF)


def on_device(
    prompt_x,
    prompt_z,
    prompt_b,
    prompt_c,
    prompt_dt,
    rate_log,
    skip_scale,
    norm_gain,
    prefix_key_rows,
    prefix_value_rows,
    fork_counts,
    fork_x,
    fork_z,
    fork_b,
    fork_c,
    fork_dt,
    fork_queries,
    fork_keys,
    branch_value_rows,
):
    slots, steps = fork_x.shape[:2]
    forks = slots * steps
    flat = lambda a: a.reshape(forks, a.shape[2])
    fx, fz, fb, fc, fdt, fq, fk, fv = map(
        flat, (fork_x, fork_z, fork_b, fork_c, fork_dt, fork_queries, fork_keys, branch_value_rows)
    )
    n_seg = lax.axis_size(SEG)
    n_tp = lax.axis_size("tp")
    tok, channels = prompt_x.shape
    heads = rate_log.shape[0]
    groups = prompt_b.shape[1] // N
    width = min(512, channels // groups)
    per_group = channels // groups // width
    tiles = channels // width
    rate, skip, gain = rate_log[None, :], skip_scale[None, :], norm_gain[None, :]
    lanes = max(128, channels // n_seg)
    lane_parts = channels // lanes
    row_parts = n_seg // lane_parts
    rows = N // row_parts
    sds = jax.ShapeDtypeStruct
    wide = pl.BlockSpec((tok, width), lambda i: (0, i))
    fwide = pl.BlockSpec((forks, width), lambda i: (0, i))
    proj = pl.BlockSpec((tok, N), lambda i: (0, i // per_group))
    fproj = pl.BlockSpec((forks, N), lambda i: (0, i // per_group))
    full = lambda *shape: pl.BlockSpec(shape, lambda i: (0,) * len(shape))
    code_spec = pl.BlockSpec((row_parts, width // lanes, rows, lanes), lambda i: (0, i, 0, 0))
    side_spec = pl.BlockSpec((row_parts, width // lanes, 8, lanes), lambda i: (0, i, 0, 0))
    code_shape = (row_parts, lane_parts, rows, lanes)
    side_shape = (row_parts, lane_parts, 8, lanes)
    sums = [VM((tok, heads), F32), VM((forks, heads), F32)]
    codes, side, pre, fpre = pl.pallas_call(
        functools.partial(first_kernel, steps, per_group),
        grid=(tiles,),
        out_shape=[sds(code_shape, jnp.int16), sds(side_shape, F32), sds((tok, channels), F32), sds((forks, channels), F32)],
        in_specs=[wide, proj, proj, full(tok, heads), full(1, heads), fwide, fproj, fproj, full(forks, heads)],
        out_specs=[code_spec, side_spec, wide, fwide],
        scratch_shapes=sums + [VM((tok, tok), BF), VM((tok, tok), BF), VM((forks, forks), F32)],
        name="first",
    )(prompt_x, prompt_b, prompt_c, prompt_dt, rate, fx, fb, fc, fdt)

    codes, side, queries = exchange(
        [codes.reshape(n_seg, rows, lanes), side.reshape(n_seg, 8, lanes), fq], (False, False, True), SEG, n_seg, 0
    )
    packed_width = fq.shape[1] + 128
    codes, side, packed = pl.pallas_call(
        functools.partial(middle_kernel, forks),
        out_shape=[sds(codes.shape, jnp.int16), sds(side.shape, F32), sds((n_seg * forks, packed_width), F32)],
        name="middle",
    )(codes, side, queries.reshape(n_seg * forks, fq.shape[1]), prefix_key_rows, prefix_value_rows)
    codes, side, packed = exchange(
        [codes, side, packed.reshape(n_seg, forks, packed_width)], (False, False, False), SEG, n_seg, 1
    )
    gated, fgated, sq = pl.pallas_call(
        functools.partial(last_kernel, steps),
        grid=(tiles,),
        out_shape=[sds((tok, channels), F32), sds((forks, channels), F32), sds((8, tok + 128), F32)],
        in_specs=[wide, wide, proj, full(tok, heads), full(1, heads), full(1, heads), fwide, fwide, fproj, full(forks, heads), code_spec, side_spec, wide, fwide],
        out_specs=[wide, fwide, full(8, tok + 128)],
        scratch_shapes=sums,
        name="last",
    )(prompt_x, prompt_z, prompt_c, prompt_dt, rate, skip, fx, fz, fc, fdt, codes.reshape(code_shape), side.reshape(side_shape), pre, fpre)
    (sq,) = exchange([sq], (True,), "tp", n_tp, 2)
    smem = pl.BlockSpec(memory_space=pltpu.SMEM)
    prompt_out, fork_mamba = pl.pallas_call(
        functools.partial(norm_kernel, steps, channels * n_tp),
        grid=(tiles,),
        out_shape=[sds((tok, channels), BF), sds((forks, channels), BF)],
        in_specs=[smem, wide, fwide, full(n_tp, 8, tok + 128), pl.BlockSpec((1, width), lambda i: (0, i))],
        out_specs=[wide, fwide],
        name="norm",
    )(fork_counts, gated, fgated, sq, gain)
    vm = pl.BlockSpec(memory_space=VM)
    fork_attn = pl.pallas_call(
        functools.partial(merge_kernel, steps),
        out_shape=sds(fq.shape, BF),
        in_specs=[smem, vm, vm, vm, vm],
        out_specs=vm,
        name="merge",
    )(fork_counts, packed, fq, fk, fv)
    shape3 = lambda a: a.reshape(slots, steps, a.shape[1])
    return (prompt_out, shape3(fork_mamba), shape3(fork_attn))


def solution(mesh):
    rows = P(SEG, "tp")
    fork = P(SEG, None, "tp")
    in_specs = (rows,) * 5 + (P("tp"),) * 3 + (rows,) * 2 + (P(SEG),) + (fork,) * 8
    return jax.shard_map(
        on_device, mesh=mesh, in_specs=in_specs, out_specs=(rows, fork, fork), check_vma=False
    )
```

```python
import functools

import jax
import jax.numpy as jnp
from jax import lax
from jax.experimental import pallas as pl
from jax.experimental.pallas import tpu as pltpu
from jax.sharding import PartitionSpec as P

P_SIZE = 64
N = 128
HEAD_DIMENSION = 128
EPSILON = 1e-05
FLOOR_SCORE = -1e30
SEG = ("ctx", "rep")
BF = jnp.bfloat16
F32 = jnp.float32
VM = pltpu.VMEM


def dot(a, b, dims=((1,), (0,))):
    return lax.dot_general(a, b, (dims, ((), ())), preferred_element_type=F32)


def split2(a):
    hi = a.astype(BF)
    return hi, (a - hi.astype(F32)).astype(BF)


def split3(a):
    hi = a.astype(BF)
    rest = a - hi.astype(F32)
    mid = rest.astype(BF)
    return hi, mid, (rest - mid.astype(F32)).astype(BF)


def mm_right(a, b, dims=((1,), (0,))):
    hi, lo = split2(b)
    return dot(a, hi, dims) + dot(a, lo, dims)


def mm_left(a, b, dims=((1,), (0,))):
    hi, lo = split2(a)
    return dot(hi, b, dims) + dot(lo, b, dims)


def mm_both(a, b):
    ah, al = split2(a)
    bh, bl = split2(b)
    return dot(ah, bh) + (dot(ah, bl) + dot(al, bh))


def iota(shape, axis):
    return lax.broadcasted_iota(jnp.int32, shape, axis)


def log2(n):
    assert n & (n - 1) == 0
    return n.bit_length() - 1


def spread(values, table):
    return mm_left(values, table)


def spread_table(heads, step, width):
    row = iota((heads, width), 0) - step * (width // P_SIZE)
    col = iota((heads, width), 1)
    return jnp.where((col >= row * P_SIZE) & (col < row * P_SIZE + P_SIZE), 1.0, 0.0).astype(BF)


def causal(rows, span):
    r, c = iota((rows, rows), 0), iota((rows, rows), 1)
    mask = r >= c
    if span < rows:
        mask = mask & ((r >> log2(span)) == (c >> log2(span)))
    return mask


def running(dt, rates, span):
    ones = jnp.where(causal(dt.shape[0], span), 1.0, 0.0).astype(BF)
    parts = split3(dt * rates)
    return dot(ones, parts[0]) + (dot(ones, parts[1]) + dot(ones, parts[2]))


def rows_of(ref):
    return jnp.concatenate([ref[i].astype(F32) for i in range(ref.shape[0])], axis=0)


def put_rows(ref, values):
    steps = ref.shape[1]
    for i in range(ref.shape[0]):
        ref[i] = values[i * steps : (i + 1) * steps].astype(ref.dtype)


def encode(chunk):
    scale = jnp.maximum(jnp.max(jnp.abs(chunk), axis=0, keepdims=True), 1e-30)
    code = jnp.floor(chunk * (32767.0 / scale) + 0.5).astype(jnp.int32).astype(jnp.int16)
    return code, scale * (1.0 / 32767.0)


def decode(code, scale):
    return code.astype(jnp.int32).astype(F32) * scale


def gate(y, z):
    z = z.astype(F32)
    return y * (z / (1.0 + jnp.exp(-z)))


def first_kernel(steps, per_group, x, b, c, dt, rate, fx, fb, fc, fdt, codes, side, pre, fpre, cum, fcum, phi, plo, fpair, fcol, grow):
    step = pl.program_id(0)
    tok, forks, heads, width = x.shape[0], fpre.shape[0], dt.shape[0], x.shape[1]

    @pl.when(step == 0)
    def _():
        rates = -jnp.exp(rate[...])
        dts = jnp.transpose(dt[...])
        cum[...] = running(dts, rates, tok)
        grow[...] = dts * jnp.exp(-cum[...])
        fcum[...] = running(rows_of(fdt), rates, steps)

    @pl.when(lax.rem(step, per_group) == 0)
    def _():
        pair = jnp.where(causal(tok, tok), dot(c[...], b[...], ((1,), (1,))), 0.0)
        phi[...], plo[...] = split2(pair)
        fcol[...] = rows_of(fc).astype(BF)
        pair = jnp.where(causal(forks, steps), dot(fcol[...], rows_of(fb).astype(BF), ((1,), (1,))), 0.0)
        fpair[...] = pair

    table = spread_table(heads, step, width)
    total = cum[...]
    xs = x[...].astype(F32) * spread(grow[...], table)
    xh, xl = split2(xs)
    pre[...] = dot(phi[...], xh) + (dot(phi[...], xl) + dot(plo[...], xh))
    last = spread(jnp.exp(total[tok - 8 :]), table)[7:8]
    state = (dot(b[...], xh, ((0,), (0,))) + dot(b[...], xl, ((0,), (0,)))) * last
    row_parts, lane_parts, rows, lanes = codes.shape
    for i in range(row_parts):
        for j in range(lane_parts):
            piece = state[i * rows : (i + 1) * rows, j * lanes : (j + 1) * lanes]
            codes[i, j], scale = encode(piece)
            side[i, j, 0:1] = scale
            side[i, j, 1:2] = last[:, j * lanes : (j + 1) * lanes]
    fxs = rows_of(fx) * spread(rows_of(fdt) * jnp.exp(-fcum[...]), table)
    sh, sl = split2(state)
    inside = mm_both(fpair[...], fxs)
    fpre[...] = inside + dot(fcol[...], sh) + dot(fcol[...], sl)


def exchange_kernel(axes, n, whole, count, *refs):
    ins, outs = refs[:count], refs[count : 2 * count]
    send, recv = refs[2 * count :]
    me = lax.axis_index(axes)

    def place(j):
        if isinstance(axes, str):
            return {axes: j}
        inner = lax.axis_size(axes[1])
        return {axes[0]: j // inner, axes[1]: lax.rem(j, inner)}

    barrier = pltpu.get_barrier_semaphore()
    for s in range(1, n):
        pl.semaphore_signal(barrier, inc=1, device_id=place(lax.rem(me + s, n)), device_id_type=pl.DeviceIdType.MESH)
    pl.semaphore_wait(barrier, n - 1)
    copies = []
    for a in range(count):
        for s in range(1, n):
            peer = lax.rem(me + s, n)
            copies.append(
                pltpu.make_async_remote_copy(
                    src_ref=ins[a] if whole[a] else ins[a].at[peer],
                    dst_ref=outs[a].at[me],
                    send_sem=send.at[a, s - 1],
                    recv_sem=recv.at[a, s - 1],
                    device_id=place(peer),
                    device_id_type=pl.DeviceIdType.MESH,
                )
            )
            copies[-1].start()
    for a in range(count):
        outs[a][me] = ins[a][...] if whole[a] else ins[a][me]
    for copy in copies:
        copy.wait()


def exchange(arrays, whole, axes, n, number):
    shapes = [
        jax.ShapeDtypeStruct(((n,) + a.shape) if w else a.shape, a.dtype) for a, w in zip(arrays, whole)
    ]
    count = len(arrays)
    spec = pl.BlockSpec(memory_space=VM)
    return pl.pallas_call(
        functools.partial(exchange_kernel, axes, n, whole, count),
        out_shape=shapes,
        in_specs=[spec] * count,
        out_specs=[spec] * count,
        scratch_shapes=[pltpu.SemaphoreType.DMA((count, n - 1)), pltpu.SemaphoreType.DMA((count, n - 1))],
        compiler_params=pltpu.CompilerParams(collective_id=number, has_side_effects=True),
        name=f"exchange{number}",
    )(*arrays)


def attend(queries, keys, values, live):
    s = dot(queries, keys, ((1,), (1,))) * (HEAD_DIMENSION ** (-0.5))
    s = jnp.where(live, s, FLOOR_SCORE)
    m = jnp.max(s, axis=1, keepdims=True)
    w = jnp.where(live, jnp.exp(s - m), 0.0)
    return mm_left(w, values), m, jnp.sum(w, axis=1, keepdims=True)


def gather_heads(queries, k, q_per):
    D = HEAD_DIMENSION
    cols = [queries[:, (k * q_per + i) * D : (k * q_per + i + 1) * D].astype(F32) for i in range(q_per)]
    return jnp.concatenate(cols, axis=0).astype(BF)


def middle_kernel(forks, codes, side, queries, keys, values, ecodes, eside, packed, extras):
    n_seg, rows, lanes = codes.shape
    D = HEAD_DIMENSION
    run = jnp.zeros((rows, lanes), F32)
    for e in range(n_seg):
        ecodes[e], scale = encode(run)
        eside[e] = scale
        run = run * side[e, 1:2] + decode(codes[e], side[e, 0:1])
    me = lax.axis_index(SEG)
    kv = keys.shape[1] // D
    q_per = queries.shape[3] // D // kv
    every = jnp.concatenate([rows_of(queries.at[e]) for e in range(n_seg)], axis=0)
    count = every.shape[0]
    shape = (q_per * count, keys.shape[0])
    live = ((iota(shape, 0) & (count - 1)) >> log2(forks)) >= me
    lane = iota((count, 128), 1)
    extra = jnp.zeros((count, 128), F32)
    for k in range(kv):
        o, m, l = attend(gather_heads(every, k, q_per), keys[:, k * D : (k + 1) * D], values[:, k * D : (k + 1) * D], live)
        scale = jnp.maximum(jnp.max(jnp.abs(o), axis=1, keepdims=True), 1e-30)
        coded = jnp.floor(o * (32767.0 / scale) + 0.5)
        scale = scale * (1.0 / 32767.0)
        for i in range(q_per):
            h = k * q_per + i
            part = slice(i * count, (i + 1) * count)
            for e in range(n_seg):
                start = i * count + e * forks
                packed[e, :, h * D : (h + 1) * D] = coded[start : start + forks].astype(jnp.int32).astype(jnp.int16)
            extra = jnp.where(lane == 2 * kv * q_per + h, scale[part], extra)
            extra = jnp.where(lane == h, m[part], extra)
            extra = jnp.where(lane == kv * q_per + h, l[part], extra)
    for e in range(n_seg):
        extras[e] = extra[e * forks : (e + 1) * forks]


def last_kernel(steps, x, z, c, dt, rate, skip, fx, fz, fc, fdt, codes, side, pre, fpre, gated, fgated, sq, cum, fcum):
    step = pl.program_id(0)
    tok, heads, width = x.shape[0], dt.shape[0], x.shape[1]

    @pl.when(step == 0)
    def _():
        rates = -jnp.exp(rate[...])
        cum[...] = jnp.exp(running(jnp.transpose(dt[...]), rates, tok))
        fcum[...] = jnp.exp(running(rows_of(fdt), rates, steps))
        sq[...] = jnp.zeros_like(sq)

    row_parts, lane_parts, rows, lanes = codes.shape
    before = jnp.concatenate(
        [
            jnp.concatenate([decode(codes[i, j], side[i, j, 0:1]) for j in range(lane_parts)], axis=1)
            for i in range(row_parts)
        ],
        axis=0,
    )
    table = spread_table(heads, step, width)
    grown = cum[...]
    fcol = rows_of(fc).astype(BF)
    wide = spread(grown, table)
    skips = spread(jnp.broadcast_to(skip[...], (8, heads)), table)[0:1]
    hi, lo = split2(before)
    y = wide * (pre[...] + (dot(c[...], hi) + dot(c[...], lo))) + skips * x[...].astype(F32)
    g = gate(y, z[...])
    gated[...] = g
    gh, gl = split2(g * g)
    ones = jnp.ones((8, width), BF)
    sq[:, :tok] += dot(ones, gh, ((1,), (1,))) + dot(ones, gl, ((1,), (1,)))
    last = spread(grown[tok - 8 :], table)[7:8]
    fy = fpre[...] + last * (dot(fcol, hi) + dot(fcol, lo))
    fg = gate(spread(fcum[...], table) * fy + skips * rows_of(fx), rows_of(fz))
    fgated[...] = fg
    sq[:, tok:] += jnp.broadcast_to(jnp.sum(fg * fg, axis=1, keepdims=True), (fg.shape[0], 128))


def norm_kernel(steps, total, counts, gated, fgated, sq, gain, out, fout):
    tok, forks = gated.shape[0], fgated.shape[0]
    sums = sq[0]
    for i in range(1, sq.shape[0]):
        sums = sums + sq[i]
    inv = lax.rsqrt(sums * (1.0 / total) + EPSILON)
    column = jnp.transpose(inv[:, :tok])[:, 0:1]
    out[...] = (gated[...] * column * gain[...]).astype(BF)
    alive = jnp.where((iota((forks, 1), 0) >> log2(steps)) < counts[0], 1.0, 0.0)
    put_rows(fout, fgated[...] * inv[:, tok : tok + 1] * gain[...] * alive)


def merge_kernel(steps, counts, packed, extra, fq, fk, fv, out):
    D = HEAD_DIMENSION
    queries, keys, values = rows_of(fq), rows_of(fk).astype(BF), rows_of(fv).astype(BF)
    forks = queries.shape[0]
    sources = packed.shape[0]
    kv = keys.shape[1] // D
    q_per = queries.shape[1] // D // kv
    heads = kv * q_per
    r = iota((q_per * forks, forks), 0) & (forks - 1)
    c = iota((q_per * forks, forks), 1)
    live = (r >= c) & ((r >> log2(steps)) == (c >> log2(steps)))
    alive = jnp.where((iota((forks, 1), 0) >> log2(steps)) < counts[0], 1.0, 0.0)
    for k in range(kv):
        o, m, l = attend(gather_heads(queries, k, q_per), keys[:, k * D : (k + 1) * D], values[:, k * D : (k + 1) * D], live)
        for i in range(q_per):
            h = k * q_per + i
            part = slice(i * forks, (i + 1) * forks)
            pk = extra[:, :, h : h + 1]
            peak = jnp.maximum(jnp.max(pk, axis=0), m[part])
            own = jnp.exp(m[part] - peak)
            total, weighted = l[part] * own, o[part] * own
            for e in range(sources):
                factor = jnp.exp(pk[e] - peak)
                total = total + extra[e, :, heads + h : heads + h + 1] * factor
                back = extra[e, :, 2 * heads + h : 2 * heads + h + 1] * factor
                weighted = weighted + decode(packed[e, :, h * D : (h + 1) * D], back)
            put_rows(out.at[:, :, h * D : (h + 1) * D], weighted / total * alive)


def on_device(
    prompt_x,
    prompt_z,
    prompt_b,
    prompt_c,
    prompt_dt,
    rate_log,
    skip_scale,
    norm_gain,
    prefix_key_rows,
    prefix_value_rows,
    fork_counts,
    fork_x,
    fork_z,
    fork_b,
    fork_c,
    fork_dt,
    fork_queries,
    fork_keys,
    branch_value_rows,
):
    slots, steps = fork_x.shape[:2]
    forks = slots * steps
    fx, fz, fb, fc, fdt, fq = fork_x, fork_z, fork_b, fork_c, fork_dt, fork_queries
    fk, fv = fork_keys, branch_value_rows
    dt = prompt_dt.T
    n_seg = lax.axis_size(SEG)
    n_tp = lax.axis_size("tp")
    tok, channels = prompt_x.shape
    heads = rate_log.shape[0]
    groups = prompt_b.shape[1] // N
    width = min(512, channels // groups)
    per_group = channels // groups // width
    tiles = channels // width
    rate, skip, gain = rate_log[None, :], skip_scale[None, :], norm_gain[None, :]
    lanes = max(128, channels // n_seg)
    lane_parts = channels // lanes
    row_parts = n_seg // lane_parts
    rows = N // row_parts
    sds = jax.ShapeDtypeStruct
    wide = pl.BlockSpec((tok, width), lambda i: (0, i))
    fwide = pl.BlockSpec((forks, width), lambda i: (0, i))
    f3 = pl.BlockSpec((slots, steps, width), lambda i: (0, 0, i))
    proj = pl.BlockSpec((tok, N), lambda i: (0, i // per_group))
    fproj = pl.BlockSpec((slots, steps, N), lambda i: (0, 0, i // per_group))
    full = lambda *shape: pl.BlockSpec(shape, lambda i: (0,) * len(shape))
    code_spec = pl.BlockSpec((row_parts, width // lanes, rows, lanes), lambda i: (0, i, 0, 0))
    side_spec = pl.BlockSpec((row_parts, width // lanes, 2, lanes), lambda i: (0, i, 0, 0))
    code_shape = (row_parts, lane_parts, rows, lanes)
    side_shape = (row_parts, lane_parts, 2, lanes)
    back_spec = pl.BlockSpec((row_parts, width // lanes, 1, lanes), lambda i: (0, i, 0, 0))
    back_shape = (row_parts, lane_parts, 1, lanes)
    sums = [VM((tok, heads), F32), VM((forks, heads), F32)]
    codes, side, pre, fpre = pl.pallas_call(
        functools.partial(first_kernel, steps, per_group),
        grid=(tiles,),
        out_shape=[sds(code_shape, jnp.int16), sds(side_shape, F32), sds((tok, channels), F32), sds((forks, channels), F32)],
        in_specs=[wide, proj, proj, full(heads, tok), full(1, heads), f3, fproj, fproj, full(slots, steps, heads)],
        out_specs=[code_spec, side_spec, wide, fwide],
        scratch_shapes=sums + [VM((tok, tok), BF), VM((tok, tok), BF), VM((forks, forks), F32), VM((forks, N), BF), VM((tok, heads), F32)],
        name="first",
    )(prompt_x, prompt_b, prompt_c, dt, rate, fx, fb, fc, fdt)

    codes, side, queries = exchange(
        [codes.reshape(n_seg, rows, lanes), side.reshape(n_seg, 2, lanes), fq], (False, False, True), SEG, n_seg, 0
    )
    codes, back, packed, extras = pl.pallas_call(
        functools.partial(middle_kernel, forks),
        out_shape=[sds(codes.shape, jnp.int16), sds((n_seg, 1, lanes), F32), sds((n_seg, forks, fq.shape[2]), jnp.int16), sds((n_seg, forks, 128), F32)],
        name="middle",
    )(codes, side, queries, prefix_key_rows, prefix_value_rows)
    codes, back, packed, extras = exchange([codes, back, packed, extras], (False,) * 4, SEG, n_seg, 1)
    gated, fgated, sq = pl.pallas_call(
        functools.partial(last_kernel, steps),
        grid=(tiles,),
        out_shape=[sds((tok, channels), F32), sds((forks, channels), F32), sds((8, tok + 128), F32)],
        in_specs=[wide, wide, proj, full(heads, tok), full(1, heads), full(1, heads), f3, f3, fproj, full(slots, steps, heads), code_spec, back_spec, wide, fwide],
        out_specs=[wide, fwide, full(8, tok + 128)],
        scratch_shapes=sums,
        name="last",
    )(prompt_x, prompt_z, prompt_c, dt, rate, skip, fx, fz, fc, fdt, codes.reshape(code_shape), back.reshape(back_shape), pre, fpre)
    (sq,) = exchange([sq], (True,), "tp", n_tp, 2)
    smem = pl.BlockSpec(memory_space=pltpu.SMEM)
    prompt_out, fork_mamba = pl.pallas_call(
        functools.partial(norm_kernel, steps, channels * n_tp),
        grid=(tiles,),
        out_shape=[sds((tok, channels), BF), sds((slots, steps, channels), BF)],
        in_specs=[smem, wide, fwide, full(n_tp, 8, tok + 128), pl.BlockSpec((1, width), lambda i: (0, i))],
        out_specs=[wide, f3],
        name="norm",
    )(fork_counts, gated, fgated, sq, gain)
    vm = pl.BlockSpec(memory_space=VM)
    fork_attn = pl.pallas_call(
        functools.partial(merge_kernel, steps),
        out_shape=sds(fq.shape, BF),
        in_specs=[smem, vm, vm, vm, vm, vm],
        out_specs=vm,
        name="merge",
    )(fork_counts, packed, extras, fq, fk, fv)
    return (prompt_out, fork_mamba, fork_attn)


def solution(mesh):
    rows = P(SEG, "tp")
    fork = P(SEG, None, "tp")
    in_specs = (rows,) * 5 + (P("tp"),) * 3 + (rows,) * 2 + (P(SEG),) + (fork,) * 8
    return jax.shard_map(
        on_device, mesh=mesh, in_specs=in_specs, out_specs=(rows, fork, fork), check_vma=False
    )
```
